128 devices in a mesh: section: 16 (over z_lo, y, core), tensor: 8 (over x, z_hi).
Axes of the slice: x: 4, y: 4, z: 4 (z_hi: 2, z_lo: 2; z = z_hi * 2 + z_lo), core: 2. Of those that a mesh axis runs over, the one named last changes fastest.
Arguments:
- inflow: bfloat16 [16, 512, 12288], P('section', 'tensor'), may hold values from -60 to 60
- fresh: bfloat16 [512, 12288], P('tensor'), may hold values from -60 to 60
- stash_held: bfloat16 [16, 512, 12288], P('section', 'tensor'), may hold values from -60 to 60
- grad_in: bfloat16 [16, 512, 12288], P('section', 'tensor'), may hold values from -6 to 6
- query_gain: float32 [16, 12288], P('section', 'tensor'), may hold values from -3 to 3
- key_gain: float32 [16, 12288], P('section', 'tensor'), may hold values from -3 to 3
- value_gain: float32 [16, 12288], P('section', 'tensor'), may hold values from -4 to 4
Outputs:
- first_out: bfloat16 [16, 512, 12288], P('section', 'tensor')
- second_out: bfloat16 [16, 512, 12288], P('section', 'tensor')
- evicted: bfloat16 [16, 512, 12288], P('section', 'tensor')
- grad_out: bfloat16 [16, 512, 12288], P('section', 'tensor')
The draws below stay inside these ranges and needn't reach their ends.
All inputs are finite; a program needn't handle non-finite values.
Results may differ from the reference program's by a relative error of at most 0.0068.
Values may be sent and summed in bfloat16 or wider, within the bound.
No kernel may reach another device: no remote copies, remote signals or barrier semaphores. Data moves between devices by JAX's collectives and lax.ppermute only.
A program may use at most 128 MiB of HBM per device.

```python
import jax
import jax.numpy as jnp
from jax import lax

D = 12288
HDIM = 128
SEQ = 512
SECTIONS = 16


def activation(base_key, leading):
    full_shape = leading + (SEQ, D)
    noise_key, row_key, col_key = jax.random.split(base_key, 3)
    noise = jax.random.truncated_normal(noise_key, -4.0, 4.0, full_shape, jnp.float32)
    row_scale = jnp.exp(jax.random.uniform(row_key, leading + (SEQ, 1), jnp.float32, -0.7, 0.7))
    col_scale = jnp.exp(jax.random.uniform(col_key, leading + (1, D), jnp.float32, -0.35, 0.35))
    result = noise * row_scale * col_scale
    return result.astype(jnp.bfloat16)


def gain_draw(base_key):
    return jax.random.truncated_normal(base_key, -3.0, 3.0, (SECTIONS, D), jnp.float32)


def draw_inflow(key, part):
    return activation(jax.random.fold_in(key, 11), (SECTIONS,))


def draw_fresh(key, part):
    return activation(jax.random.fold_in(key, 12), ())


def draw_stash_held(key, part):
    return activation(jax.random.fold_in(key, 13), (SECTIONS,))


def draw_query_gain(key, part):
    return gain_draw(jax.random.fold_in(key, 21))


def draw_key_gain(key, part):
    return gain_draw(jax.random.fold_in(key, 22))


def block_scale(own_key, extent, cuts, low, high):
    gain = 1.0
    for dim, shards_of in cuts:
        steps = jax.random.uniform(jax.random.fold_in(jax.random.fold_in(own_key, 6), dim), (shards_of,), jnp.float32, low / len(cuts), high / len(cuts))
        gain = gain * jnp.repeat(jnp.exp(steps), extent[dim] // shards_of).reshape((-1,) + (1,) * (len(extent) - 1 - dim))
    return gain


def normal_values(key, dims, spread, bound, pieces=(), dtype=jnp.bfloat16):
    drawn = jax.random.normal(key, dims, jnp.float32) * spread
    if len(pieces) > 0:
        drawn = block_scale(key, dims, pieces, -0.22, 0.18) * drawn
    return jnp.clip(drawn, min=-bound, max=bound).astype(dtype)


def setup_inputs(seed: int = 0) -> dict:
    splits = jax.random.split(jax.random.key(seed), 8)
    return {
        "inflow": draw_inflow(jax.random.fold_in(splits[7], 71), 0),
        "fresh": draw_fresh(jax.random.fold_in(splits[7], 71), 0),
        "stash_held": draw_stash_held(jax.random.fold_in(splits[7], 71), 0),
        "grad_in": normal_values(splits[3], (SECTIONS, SEQ, D), 1.0, 6.0, ((0, 16), (1, 8))),
        "query_gain": draw_query_gain(jax.random.fold_in(splits[7], 71), 0),
        "key_gain": draw_key_gain(jax.random.fold_in(splits[7], 71), 0),
        "value_gain": normal_values(splits[6], (SECTIONS, D), 1.0, 4.0, ((0, 16), (1, 8)), jnp.float32),
    }


epsilon = 1e-05
masked_score = -1e+30

def rounded(values):
    return lax.optimization_barrier(values.astype(jnp.bfloat16)).astype(jnp.float32)

def normalize(tokens_in):
    values = tokens_in.astype(jnp.float32)
    factor = lax.rsqrt(lax.optimization_barrier(jnp.mean(values * values, axis=-1, keepdims=True)) + epsilon)
    return (values * factor, factor)

def heads_of(normed, feature_gain):
    scaled = rounded(normed * feature_gain)
    return scaled.reshape(scaled.shape[0], -1, HDIM)

def softmax_causal(queries, key_heads):
    scores = jnp.einsum('ihd,jhd->hij', queries, key_heads) * HDIM ** (-0.5)
    length = queries.shape[0]
    row_index = lax.broadcasted_iota(jnp.int32, (length, length), 0)
    col_index = lax.broadcasted_iota(jnp.int32, (length, length), 1)
    scores = jnp.where(row_index >= col_index, scores, masked_score)
    largest = lax.optimization_barrier(jnp.max(scores, axis=-1, keepdims=True))
    weights = jnp.exp(scores - largest)
    return weights / lax.optimization_barrier(jnp.sum(weights, axis=-1, keepdims=True))

def layer_forward(section_in):
    tokens_in, query_gain, key_gain, value_gain = section_in
    scaled, factor = normalize(tokens_in)
    normed = rounded(scaled)
    queries = heads_of(normed, query_gain)
    key_heads = heads_of(normed, key_gain)
    value_heads = heads_of(normed, value_gain)
    weights = rounded(softmax_causal(queries, key_heads))
    mixed_out = jnp.einsum('hij,jhd->ihd', weights, value_heads)
    mixed_out = rounded(mixed_out.reshape(tokens_in.shape))
    return (tokens_in.astype(jnp.float32) + mixed_out).astype(jnp.bfloat16)

def layer_backward(section_in):
    stash_rows, grad_rows, query_gain, key_gain, value_gain = section_in
    scaled, factor = normalize(stash_rows)
    normed = rounded(scaled)
    queries = heads_of(normed, query_gain)
    key_heads = heads_of(normed, key_gain)
    value_heads = heads_of(normed, value_gain)
    grad_values = grad_rows.astype(jnp.float32)
    cotangent = grad_values.reshape(grad_values.shape[0], -1, HDIM)
    weights = softmax_causal(queries, key_heads)
    weights_low = rounded(weights)
    value_grad = jnp.einsum('hij,ihd->jhd', weights_low, cotangent)
    prob_grad = jnp.einsum('ihd,jhd->hij', cotangent, value_heads)
    score_grad = weights * (prob_grad - lax.optimization_barrier(jnp.sum(prob_grad * weights, axis=-1, keepdims=True)))
    score_low = rounded(score_grad)
    query_grad = jnp.einsum('hij,jhd->ihd', score_low, key_heads) * HDIM ** (-0.5)
    key_grad = jnp.einsum('hij,ihd->jhd', score_low, queries) * HDIM ** (-0.5)
    full_shape = stash_rows.shape
    normed_grad = query_grad.reshape(full_shape) * query_gain + key_grad.reshape(full_shape) * key_gain
    normed_grad = rounded(normed_grad + value_grad.reshape(full_shape) * value_gain)
    inner = lax.optimization_barrier(jnp.mean(normed_grad * scaled, axis=-1, keepdims=True))
    return (grad_values + factor * (normed_grad - scaled * inner)).astype(jnp.bfloat16)

def reference(inflow, fresh, stash_held, grad_in, query_gain, key_gain, value_gain):
    first_out = lax.map(layer_forward, (inflow, query_gain, key_gain, value_gain))
    second_in = jnp.concatenate([fresh[None], first_out[:-1]], axis=0)
    second_out = lax.map(layer_forward, (second_in, query_gain, key_gain, value_gain))
    stash = stash_held[::-1]
    grad_out = lax.map(layer_backward, (stash, grad_in, query_gain, key_gain, value_gain))
    evicted = inflow[::-1]
    return (first_out, second_out, evicted, grad_out)
```

```python
import math

import jax
import jax.numpy as jnp
from jax import lax
from jax.experimental import pallas as pl
from jax.experimental.pallas import tpu as pltpu
from jax.sharding import PartitionSpec as P

D = 12288
HDIM = 128
SEQ = 512
SECTIONS = 16
PEERS = 8
TOK = SEQ // PEERS
HEADS = D // HDIM // PEERS
FEAT = HEADS * HDIM
ROWS = HEADS * TOK
MSG = ROWS + 8
QB = 128
EPS = 1e-05
NEG = -1e30
SCALE = HDIM**-0.5
EXPC = SCALE * math.log2(math.e)
BF = jnp.bfloat16
F32 = jnp.float32
BOTH = ("section", "tensor")
VMEM = pl.BlockSpec(memory_space=pltpu.VMEM)
SMEM = pl.BlockSpec(memory_space=pltpu.SMEM)


def dot(a, b, ca, cb, precision=None):
    return lax.dot_general(
        a, b, (((ca,), (cb,)), ((), ())), precision=precision, preferred_element_type=F32
    )


def stats_tile(x_ref):
    acc = jnp.zeros((TOK, HDIM), F32)
    for c in range(D // HDIM):
        v = x_ref[:, c * HDIM : (c + 1) * HDIM].astype(F32)
        acc = acc + v * v
    total = dot(jnp.ones((8, HDIM), F32), acc, 1, 1, lax.Precision.HIGHEST)
    hi = total.astype(BF).astype(F32)
    mid = (total - hi).astype(BF).astype(F32)
    low = total - hi - mid
    row = lax.broadcasted_iota(jnp.int32, (8, TOK), 0)
    pieces = jnp.where(row == 0, hi, jnp.where(row == 1, mid, jnp.where(row == 2, low, 0.0)))
    return jnp.concatenate([pieces, jnp.zeros((8, HDIM - TOK), F32)], axis=1).astype(BF)


def pack_natural_kernel(x_ref, out_ref, *, stats):
    for u in range(PEERS):
        for h in range(HEADS):
            c = u * FEAT + h * HDIM
            out_ref[u, h * TOK : (h + 1) * TOK, :] = x_ref[:, c : c + HDIM]
    if stats:
        tile = stats_tile(x_ref)
        for u in range(PEERS):
            out_ref[u, ROWS:MSG, :] = tile


def pack_xor_kernel(t_ref, x_ref, *outs):
    t = t_ref[0]
    tile = stats_tile(x_ref)
    for k in range(PEERS):
        base = (t ^ k) * FEAT
        for h in range(HEADS):
            c = pl.multiple_of(base + h * HDIM, HDIM)
            outs[k][h * TOK : (h + 1) * TOK, :] = x_ref[:, pl.ds(c, HDIM)]
        outs[k][ROWS:MSG, :] = tile


def pack_natural(x, stats):
    rows = MSG if stats else ROWS

    def body(x_ref, out_ref):
        pack_natural_kernel(x_ref, out_ref, stats=stats)

    return pl.pallas_call(
        body,
        out_shape=jax.ShapeDtypeStruct((PEERS, rows, HDIM), BF),
        in_specs=[VMEM],
        out_specs=VMEM,
        name="pack_natural",
    )(x)


def pack_xor(t, x):
    return pl.pallas_call(
        pack_xor_kernel,
        out_shape=[jax.ShapeDtypeStruct((MSG, HDIM), BF)] * PEERS,
        in_specs=[SMEM, VMEM],
        out_specs=[VMEM] * PEERS,
        name="pack_xor",
    )(t, x)


def unpack_natural_kernel(m_ref, out_ref):
    for u in range(PEERS):
        for h in range(HEADS):
            c = u * FEAT + h * HDIM
            out_ref[0, :, c : c + HDIM] = m_ref[u, h * TOK : (h + 1) * TOK, :]


def unpack_xor_kernel(t_ref, *refs):
    t = t_ref[0]
    out_ref = refs[PEERS]
    for k in range(PEERS):
        base = (t ^ k) * FEAT
        for h in range(HEADS):
            c = pl.multiple_of(base + h * HDIM, HDIM)
            out_ref[0, :, pl.ds(c, HDIM)] = refs[k][h * TOK : (h + 1) * TOK, :]


def unpack_natural(m):
    return pl.pallas_call(
        unpack_natural_kernel,
        out_shape=jax.ShapeDtypeStruct((1, TOK, D), BF),
        in_specs=[VMEM],
        out_specs=VMEM,
        name="unpack_natural",
    )(m)


def unpack_xor(t, ms):
    return pl.pallas_call(
        unpack_xor_kernel,
        out_shape=jax.ShapeDtypeStruct((1, TOK, D), BF),
        in_specs=[SMEM] + [VMEM] * PEERS,
        out_specs=VMEM,
        name="unpack_xor",
    )(t, *ms)


def factor_column(tile):
    ones = jnp.ones((8, HDIM), BF)
    total = dot(tile, ones, 0, 0)
    return lax.rsqrt(total[:TOK] * (1.0 / D) + EPS)


def column_of_rows(rows):
    return dot(rows, jnp.full((8, HDIM), 0.125, F32), 0, 0, lax.Precision.HIGHEST)


def heads_of(x, factor, qg, kg, vg):
    scaled = x * factor
    normed = scaled.astype(BF).astype(F32)
    return scaled, (normed * qg).astype(BF), (normed * kg).astype(BF), (normed * vg).astype(BF)


def probs_block(q, k, i):
    n = (i + 1) * QB
    s = dot(q[i * QB : n], k[:n], 1, 1)
    row = lax.broadcasted_iota(jnp.int32, (QB, QB), 0)
    col = lax.broadcasted_iota(jnp.int32, (QB, QB), 1)
    last = jnp.where(row >= col, s[:, i * QB :], NEG)
    s = jnp.concatenate([s[:, : i * QB], last], axis=1) if i else last
    e = jnp.exp2((s - jnp.max(s, axis=1, keepdims=True)) * EXPC)
    return e * (1.0 / jnp.sum(e, axis=1, keepdims=True))


def attend(x, factor, qg, kg, vg, store):
    _, q, k, v = heads_of(x, factor, qg, kg, vg)
    for i in range(SEQ // QB):
        n = (i + 1) * QB
        p = probs_block(q, k, i).astype(BF)
        mixed = dot(p, v[:n], 1, 0).astype(BF).astype(F32)
        store(i, (x[i * QB : n] + mixed).astype(BF))


def first_kernel(x_ref, tile_ref, qg_ref, kg_ref, vg_ref, y_ref, ss_ref, factor_scr, sq_scr):
    h = pl.program_id(0)

    @pl.when(h == 0)
    def _():
        for u in range(PEERS):
            factor_scr[u * TOK : (u + 1) * TOK, :] = factor_column(tile_ref[u])
        sq_scr[...] = jnp.zeros_like(sq_scr)

    x = x_ref[...].reshape(SEQ, HDIM).astype(F32)

    def store(i, y):
        per = QB // TOK
        y_ref[i * per : (i + 1) * per] = y.reshape(per, TOK, HDIM)
        yf = y.astype(F32)
        sq_scr[i * QB : (i + 1) * QB, :] += yf * yf

    attend(x, factor_scr[...], qg_ref[...], kg_ref[...], vg_ref[...], store)

    @pl.when(h == HEADS - 1)
    def _():
        ss_ref[...] = dot(jnp.ones((8, HDIM), F32), sq_scr[...], 1, 1, lax.Precision.HIGHEST)


GAIN = pl.BlockSpec((1, HDIM), lambda h, *_: (0, h))
HEADBLK = pl.BlockSpec((PEERS, TOK, HDIM), lambda h, *_: (0, h, 0))
TILES = pl.BlockSpec((PEERS, 8, HDIM), lambda h, *_: (0, ROWS // 8, 0))
ROWSPEC = pl.BlockSpec((8, SEQ), lambda h, *_: (0, 0))
MSGHEAD = pl.BlockSpec((TOK, HDIM), lambda h, *_: (h, 0))
MSGTILE = pl.BlockSpec((8, HDIM), lambda h, *_: (ROWS // 8, 0))


def first_layer(xm, qg, kg, vg):
    return pl.pallas_call(
        first_kernel,
        grid=(HEADS,),
        in_specs=[HEADBLK, TILES, GAIN, GAIN, GAIN],
        out_specs=[HEADBLK, ROWSPEC],
        out_shape=[
            jax.ShapeDtypeStruct((PEERS, ROWS, HDIM), BF),
            jax.ShapeDtypeStruct((8, SEQ), F32),
        ],
        scratch_shapes=[pltpu.VMEM((SEQ, HDIM), F32), pltpu.VMEM((SEQ, HDIM), F32)],
        name="first_layer",
    )(xm, xm, qg, kg, vg)


def second_kernel(
    meta_ref, y_ref, ss_ref, qg_ref, kg_ref, vg_ref, *rest
):
    fresh = rest[:PEERS]
    tiles = rest[PEERS : 2 * PEERS]
    outs = rest[2 * PEERS : 3 * PEERS]
    x_scr, out_scr, factor_scr = rest[3 * PEERS :]
    h = pl.program_id(0)
    t = meta_ref[0]
    last = meta_ref[1] == 1

    @pl.when(h == 0)
    def _():
        factor_scr[...] = lax.rsqrt(column_of_rows(ss_ref[...]) * (1.0 / D) + EPS)

    @pl.when(jnp.logical_and(h == 0, last))
    def _():
        for k in range(PEERS):
            at = pl.multiple_of((t ^ k) * TOK, TOK)
            factor_scr[pl.ds(at, TOK), :] = factor_column(tiles[k][...])

    @pl.when(jnp.logical_not(last))
    def _():
        x_scr[...] = y_ref[...]

    @pl.when(last)
    def _():
        for k in range(PEERS):
            x_scr[t ^ k] = fresh[k][...]

    x = x_scr[...].reshape(SEQ, HDIM).astype(F32)

    def store(i, y):
        per = QB // TOK
        out_scr[i * per : (i + 1) * per] = y.reshape(per, TOK, HDIM)

    attend(x, factor_scr[...], qg_ref[...], kg_ref[...], vg_ref[...], store)
    for k in range(PEERS):
        outs[k][...] = out_scr[t ^ k]


def second_layer(meta, y, ss, qg, kg, vg, fresh):
    return pl.pallas_call(
        second_kernel,
        grid_spec=pltpu.PrefetchScalarGridSpec(
            num_scalar_prefetch=1,
            grid=(HEADS,),
            in_specs=[HEADBLK, ROWSPEC, GAIN, GAIN, GAIN] + [MSGHEAD] * PEERS + [MSGTILE] * PEERS,
            out_specs=[MSGHEAD] * PEERS,
            scratch_shapes=[
                pltpu.VMEM((PEERS, TOK, HDIM), BF),
                pltpu.VMEM((PEERS, TOK, HDIM), BF),
                pltpu.VMEM((SEQ, HDIM), F32),
            ],
        ),
        out_shape=[jax.ShapeDtypeStruct((ROWS, HDIM), BF)] * PEERS,
        name="second_layer",
    )(meta, y, ss, qg, kg, vg, *fresh, *fresh)


def backward_kernel(meta_ref, g_ref, qg_ref, kg_ref, vg_ref, *rest):
    msgs = rest[:PEERS]
    tiles = rest[PEERS : 2 * PEERS]
    dn_ref, x_ref, factor_ref, in_ref = rest[2 * PEERS : 2 * PEERS + 4]
    in_scr, p_scr, ds_scr = rest[2 * PEERS + 4 :]
    h = pl.program_id(0)
    t = meta_ref[0]

    @pl.when(h == 0)
    def _():
        for k in range(PEERS):
            at = pl.multiple_of((t ^ k) * TOK, TOK)
            factor_ref[pl.ds(at, TOK), :] = factor_column(tiles[k][...])
        in_scr[...] = jnp.zeros_like(in_scr)

    for k in range(PEERS):
        x_ref[t ^ k] = msgs[k][...]
    x = x_ref[...].reshape(SEQ, HDIM).astype(F32)
    g = g_ref[...].reshape(SEQ, HDIM)
    scaled, q, k, v = heads_of(x, factor_ref[...], qg_ref[...], kg_ref[...], vg_ref[...])
    dq = []
    for i in range(SEQ // QB):
        n = (i + 1) * QB
        p = probs_block(q, k, i)
        p_scr[i * QB : n, :n] = p.astype(BF)
        dp = dot(g[i * QB : n], v[:n], 1, 1)
        ds = (p * (dp - jnp.sum(dp * p, axis=1, keepdims=True))).astype(BF)
        ds_scr[i * QB : n, :n] = ds
        dq.append(dot(ds, k[:n], 1, 0))
    per = QB // TOK
    for j in range(SEQ // QB):
        lo, hi = j * QB, (j + 1) * QB
        dv = dot(p_scr[lo:, lo:hi], g[lo:], 0, 0)
        dk = dot(ds_scr[lo:, lo:hi], q[lo:], 0, 0)
        dn = dq[j] * SCALE * qg_ref[...] + dk * SCALE * kg_ref[...] + dv * vg_ref[...]
        dn = dn.astype(BF)
        dn_ref[j * per : (j + 1) * per] = dn.reshape(per, TOK, HDIM)
        in_scr[lo:hi, :] += dn.astype(F32) * scaled[lo:hi]

    @pl.when(h == HEADS - 1)
    def _():
        in_ref[...] = dot(jnp.ones((8, HDIM), F32), in_scr[...], 1, 1, lax.Precision.HIGHEST)


def backward_heads(meta, g, msgs, qg, kg, vg):
    return pl.pallas_call(
        backward_kernel,
        grid_spec=pltpu.PrefetchScalarGridSpec(
            num_scalar_prefetch=1,
            grid=(HEADS,),
            in_specs=[HEADBLK, GAIN, GAIN, GAIN] + [MSGHEAD] * PEERS + [MSGTILE] * PEERS,
            out_specs=[
                HEADBLK,
                HEADBLK,
                pl.BlockSpec((SEQ, HDIM), lambda h, *_: (0, 0)),
                ROWSPEC,
            ],
            scratch_shapes=[
                pltpu.VMEM((SEQ, HDIM), F32),
                pltpu.VMEM((SEQ, SEQ), BF),
                pltpu.VMEM((SEQ, SEQ), BF),
            ],
        ),
        out_shape=[
            jax.ShapeDtypeStruct((PEERS, ROWS, HDIM), BF),
            jax.ShapeDtypeStruct((PEERS, ROWS, HDIM), BF),
            jax.ShapeDtypeStruct((SEQ, HDIM), F32),
            jax.ShapeDtypeStruct((8, SEQ), F32),
        ],
        name="backward_heads",
    )(meta, g, qg, kg, vg, *msgs, *msgs)


def finish_kernel(g_ref, dn_ref, x_ref, factor_ref, in_ref, out_ref, inner_scr):
    @pl.when(pl.program_id(0) == 0)
    def _():
        inner_scr[...] = column_of_rows(in_ref[...]) * (1.0 / D)

    factor = factor_ref[...]
    a = x_ref[...].reshape(SEQ, HDIM).astype(F32) * factor
    dn = dn_ref[...].reshape(SEQ, HDIM).astype(F32)
    g = g_ref[...].reshape(SEQ, HDIM).astype(F32)
    out = (g + factor * (dn - a * inner_scr[...])).astype(BF)
    out_ref[...] = out.reshape(PEERS, TOK, HDIM)


def finish(g, dn, x, factor, inner):
    return pl.pallas_call(
        finish_kernel,
        grid=(HEADS,),
        in_specs=[
            HEADBLK,
            HEADBLK,
            HEADBLK,
            pl.BlockSpec((SEQ, HDIM), lambda h: (0, 0)),
            ROWSPEC,
        ],
        out_specs=HEADBLK,
        out_shape=jax.ShapeDtypeStruct((PEERS, ROWS, HDIM), BF),
        scratch_shapes=[pltpu.VMEM((SEQ, HDIM), F32)],
        name="finish",
    )(g, dn, x, factor, inner)


def exchange(m):
    return lax.all_to_all(m, "tensor", split_axis=0, concat_axis=0, tiled=True)


def xor_moves(msgs, target, sources=range(SECTIONS)):
    out = []
    for k in range(PEERS):
        pairs = [
            (s * PEERS + t, target(s) * PEERS + (t ^ k)) for s in sources for t in range(PEERS)
        ]
        if all(a == b for a, b in pairs):
            out.append(msgs[k])
        else:
            out.append(lax.ppermute(msgs[k], BOTH, pairs))
    return out


def all_sum(v):
    for mask in (1, 2, 4):
        v = v + lax.ppermute(v, "tensor", [(t, t ^ mask) for t in range(PEERS)])
    return v


def per_device(inflow, fresh, stash_held, grad_in, query_gain, key_gain, value_gain):
    t = lax.axis_index("tensor").astype(jnp.int32)
    last = (lax.axis_index("section") == SECTIONS - 1).astype(jnp.int32)
    tvec = t[None]
    meta = jnp.stack([t, last])
    gains = jnp.concatenate([query_gain, key_gain, value_gain], axis=0)
    ahead = lax.ppermute(
        gains, "section", [((s + 1) % SECTIONS, s) for s in range(SECTIONS)]
    )
    here = (query_gain, key_gain, value_gain)
    following = (ahead[0:1], ahead[1:2], ahead[2:3])

    xm = exchange(pack_natural(inflow[0], True))
    stash_msgs = xor_moves(pack_xor(tvec, stash_held[0]), lambda s: SECTIONS - 1 - s)
    gm = exchange(pack_natural(grad_in[0], False))
    fresh_msgs = xor_moves(pack_xor(tvec, fresh), lambda s: s, (SECTIONS - 1,))
    evicted = lax.ppermute(
        inflow, "section", [(s, SECTIONS - 1 - s) for s in range(SECTIONS)]
    )

    y, ss = first_layer(xm, *here)
    first_out = unpack_natural(exchange(y))
    out_msgs = second_layer(meta, y, all_sum(ss), *following, fresh_msgs)
    second_out = unpack_xor(tvec, xor_moves(out_msgs, lambda s: (s + 1) % SECTIONS))

    dn, xn, factor, inner = backward_heads(meta, gm, stash_msgs, *here)
    grad_out = unpack_natural(exchange(finish(gm, dn, xn, factor, all_sum(inner))))
    return (first_out, second_out, evicted, grad_out)


def solution(mesh):
    rows = P("section", "tensor", None)
    gain = P("section", "tensor")
    return jax.shard_map(
        per_device,
        mesh=mesh,
        in_specs=(rows, P("tensor", None), rows, rows, gain, gain, gain),
        out_specs=(rows, rows, rows, rows),
        check_vma=False,
    )
```

```python
import math

import jax
import jax.numpy as jnp
from jax import lax
from jax.experimental import pallas as pl
from jax.experimental.pallas import tpu as pltpu
from jax.sharding import PartitionSpec as P


D = 12288
HDIM = 128
SEQ = 512
SECTIONS = 16
PEERS = 8
TOK = SEQ // PEERS
HEADS = D // HDIM // PEERS
FEAT = HEADS * HDIM
ROWS = HEADS * TOK
MSG = ROWS + 8
WIDE = 2 * ROWS + 8
QB = 512
HG = 4
FG = 6
MIB = 1 << 20
EPS = 1e-05
NEG = -1e30
SCALE = HDIM**-0.5
EXPC = SCALE * math.log2(math.e)
BF = jnp.bfloat16
F32 = jnp.float32
BOTH = ("section", "tensor")
VMEM = pl.BlockSpec(memory_space=pltpu.VMEM)
SMEM = pl.BlockSpec(memory_space=pltpu.SMEM)


def dot(a, b, ca, cb, precision=None):
    return lax.dot_general(
        a, b, (((ca,), (cb,)), ((), ())), precision=precision, preferred_element_type=F32
    )


def stats_tile(x_ref):
    acc = jnp.zeros((TOK, HDIM), F32)
    for c in range(D // HDIM):
        v = x_ref[:, c * HDIM : (c + 1) * HDIM].astype(F32)
        acc = acc + v * v
    total = dot(jnp.ones((8, HDIM), F32), acc, 1, 1, lax.Precision.HIGHEST)
    hi = total.astype(BF).astype(F32)
    mid = (total - hi).astype(BF).astype(F32)
    low = total - hi - mid
    row = lax.broadcasted_iota(jnp.int32, (8, TOK), 0)
    pieces = jnp.where(row == 0, hi, jnp.where(row == 1, mid, jnp.where(row == 2, low, 0.0)))
    return jnp.concatenate([pieces, jnp.zeros((8, HDIM - TOK), F32)], axis=1).astype(BF)


def pack_wide_kernel(x_ref, g_ref, out_ref):
    for u in range(PEERS):
        for h in range(HEADS):
            c = u * FEAT + h * HDIM
            out_ref[u, h * TOK : (h + 1) * TOK, :] = x_ref[:, c : c + HDIM]
            out_ref[u, ROWS + h * TOK : ROWS + (h + 1) * TOK, :] = g_ref[:, c : c + HDIM]
    tile = stats_tile(x_ref)
    for u in range(PEERS):
        out_ref[u, 2 * ROWS : WIDE, :] = tile


def pack_xor_kernel(t_ref, x_ref, *outs):
    t = t_ref[0]
    tile = stats_tile(x_ref)
    for k in range(PEERS):
        base = (t ^ k) * FEAT
        for h in range(HEADS):
            c = pl.multiple_of(base + h * HDIM, HDIM)
            outs[k][h * TOK : (h + 1) * TOK, :] = x_ref[:, pl.ds(c, HDIM)]
        outs[k][ROWS:MSG, :] = tile


def pack_wide(x, g):
    return pl.pallas_call(
        pack_wide_kernel,
        out_shape=jax.ShapeDtypeStruct((PEERS, WIDE, HDIM), BF),
        in_specs=[VMEM, VMEM],
        out_specs=VMEM,
        compiler_params=pltpu.CompilerParams(vmem_limit_bytes=12 * MIB),
        name="pack_wide",
    )(x, g)


def pack_xor(t, x):
    return pl.pallas_call(
        pack_xor_kernel,
        out_shape=[jax.ShapeDtypeStruct((MSG, HDIM), BF)] * PEERS,
        in_specs=[SMEM, VMEM],
        out_specs=[VMEM] * PEERS,
        compiler_params=pltpu.CompilerParams(vmem_limit_bytes=8 * MIB),
        name="pack_xor",
    )(t, x)


def unpack_natural_kernel(m_ref, out_ref):
    for u in range(PEERS):
        for h in range(HEADS):
            c = u * FEAT + h * HDIM
            out_ref[0, :, c : c + HDIM] = m_ref[u, h * TOK : (h + 1) * TOK, :]


def unpack_xor_kernel(t_ref, *refs):
    t = t_ref[0]
    out_ref = refs[PEERS]
    for k in range(PEERS):
        base = (t ^ k) * FEAT
        for h in range(HEADS):
            c = pl.multiple_of(base + h * HDIM, HDIM)
            out_ref[0, :, pl.ds(c, HDIM)] = refs[k][h * TOK : (h + 1) * TOK, :]


def unpack_natural(m):
    return pl.pallas_call(
        unpack_natural_kernel,
        out_shape=jax.ShapeDtypeStruct((1, TOK, D), BF),
        in_specs=[VMEM],
        out_specs=VMEM,
        compiler_params=pltpu.CompilerParams(vmem_limit_bytes=8 * MIB),
        name="unpack_natural",
    )(m)


def unpack_xor(t, ms):
    return pl.pallas_call(
        unpack_xor_kernel,
        out_shape=jax.ShapeDtypeStruct((1, TOK, D), BF),
        in_specs=[SMEM] + [VMEM] * PEERS,
        out_specs=VMEM,
        compiler_params=pltpu.CompilerParams(vmem_limit_bytes=8 * MIB),
        name="unpack_xor",
    )(t, *ms)


def factor_column(tile):
    ones = jnp.ones((8, HDIM), BF)
    total = dot(tile, ones, 0, 0)
    return lax.rsqrt(total[:TOK] * (1.0 / D) + EPS)


def column_of_rows(rows):
    return dot(rows, jnp.full((8, HDIM), 0.125, F32), 0, 0, lax.Precision.HIGHEST)


def heads_of(x, factor, qg, kg, vg):
    scaled = x * factor
    normed = scaled.astype(BF).astype(F32)
    return scaled, (normed * qg).astype(BF), (normed * kg).astype(BF), (normed * vg).astype(BF)


def probs_block(q, k, i):
    n = (i + 1) * QB
    s = dot(q[i * QB : n], k[:n], 1, 1)
    row = lax.broadcasted_iota(jnp.int32, (QB, QB), 0)
    col = lax.broadcasted_iota(jnp.int32, (QB, QB), 1)
    last = jnp.where(row >= col, s[:, i * QB :], NEG)
    s = jnp.concatenate([s[:, : i * QB], last], axis=1) if i else last
    e = jnp.exp2((s - jnp.max(s, axis=1, keepdims=True)) * EXPC)
    return e * (1.0 / jnp.sum(e, axis=1, keepdims=True))


def attend(x, factor, qg, kg, vg, store):
    _, q, k, v = heads_of(x, factor, qg, kg, vg)
    for i in range(SEQ // QB):
        n = (i + 1) * QB
        p = probs_block(q, k, i).astype(BF)
        mixed = dot(p, v[:n], 1, 0).astype(BF).astype(F32)
        store(i, (x[i * QB : n] + mixed).astype(BF))


def first_kernel(x_ref, tile_ref, qg_ref, kg_ref, vg_ref, y_ref, ss_ref, factor_scr, sq_scr):
    h = pl.program_id(0)

    @pl.when(h == 0)
    def _():
        for u in range(PEERS):
            factor_scr[u * TOK : (u + 1) * TOK, :] = factor_column(tile_ref[u])
        sq_scr[...] = jnp.zeros_like(sq_scr)

    for b in range(HG):
        rows, lanes = slice(b * TOK, (b + 1) * TOK), slice(b * HDIM, (b + 1) * HDIM)
        x = x_ref[:, rows, :].reshape(SEQ, HDIM).astype(F32)

        def store(i, y):
            per = QB // TOK
            y_ref[i * per : (i + 1) * per, rows, :] = y.reshape(per, TOK, HDIM)
            yf = y.astype(F32)
            sq_scr[i * QB : (i + 1) * QB, :] += yf * yf

        attend(x, factor_scr[...], qg_ref[:, lanes], kg_ref[:, lanes], vg_ref[:, lanes], store)

    @pl.when(h == HEADS // HG - 1)
    def _():
        ss_ref[...] = dot(jnp.ones((8, HDIM), F32), sq_scr[...], 1, 1, lax.Precision.HIGHEST)


def gain_spec():
    return pl.BlockSpec((1, HG * HDIM), lambda h, *_: (0, h))


def head_spec(per, skip=0):
    first = skip // per
    return pl.BlockSpec((PEERS, per * TOK, HDIM), lambda h, *_: (0, first + h, 0))


def message_spec():
    return pl.BlockSpec((HG * TOK, HDIM), lambda h, *_: (h, 0))


TILES = pl.BlockSpec((PEERS, 8, HDIM), lambda h, *_: (0, 2 * ROWS // 8, 0))
ROWSPEC = pl.BlockSpec((8, SEQ), lambda h, *_: (0, 0))
SECONDROWS = pl.BlockSpec((8, SEQ), lambda h, *_: (1, 0))
BOTHROWS = pl.BlockSpec((16, SEQ), lambda h, *_: (0, 0))
MSGTILE = pl.BlockSpec((8, HDIM), lambda h, *_: (ROWS // 8, 0))


def first_layer(xm, qg, kg, vg):
    return pl.pallas_call(
        first_kernel,
        grid=(HEADS // HG,),
        in_specs=[head_spec(HG), TILES, gain_spec(), gain_spec(), gain_spec()],
        out_specs=[head_spec(HG), ROWSPEC],
        out_shape=[
            jax.ShapeDtypeStruct((PEERS, ROWS, HDIM), BF),
            jax.ShapeDtypeStruct((8, SEQ), F32),
        ],
        scratch_shapes=[pltpu.VMEM((SEQ, HDIM), F32), pltpu.VMEM((SEQ, HDIM), F32)],
        compiler_params=pltpu.CompilerParams(vmem_limit_bytes=24 * MIB),
        name="first_layer",
    )(xm, xm, qg, kg, vg)


def second_kernel(
    meta_ref, y_ref, ss_ref, qg_ref, kg_ref, vg_ref, *rest
):
    fresh = rest[:PEERS]
    tiles = rest[PEERS : 2 * PEERS]
    outs = rest[2 * PEERS : 3 * PEERS]
    x_scr, out_scr, factor_scr = rest[3 * PEERS :]
    h = pl.program_id(0)
    t = meta_ref[0]
    last = meta_ref[1] == 1

    @pl.when(h == 0)
    def _():
        factor_scr[...] = lax.rsqrt(column_of_rows(ss_ref[...]) * (1.0 / D) + EPS)

    @pl.when(jnp.logical_and(h == 0, last))
    def _():
        for k in range(PEERS):
            at = pl.multiple_of((t ^ k) * TOK, TOK)
            factor_scr[pl.ds(at, TOK), :] = factor_column(tiles[k][...])

    @pl.when(jnp.logical_not(last))
    def _():
        x_scr[...] = y_ref[...]

    @pl.when(last)
    def _():
        for k in range(PEERS):
            x_scr[t ^ k] = fresh[k][...]

    for b in range(HG):
        rows, lanes = slice(b * TOK, (b + 1) * TOK), slice(b * HDIM, (b + 1) * HDIM)
        x = x_scr[:, rows, :].reshape(SEQ, HDIM).astype(F32)

        def store(i, y):
            per = QB // TOK
            out_scr[i * per : (i + 1) * per, rows, :] = y.reshape(per, TOK, HDIM)

        attend(x, factor_scr[...], qg_ref[:, lanes], kg_ref[:, lanes], vg_ref[:, lanes], store)
    for k in range(PEERS):
        outs[k][...] = out_scr[t ^ k]


def second_layer(meta, y, ss, qg, kg, vg, fresh):
    return pl.pallas_call(
        second_kernel,
        grid_spec=pltpu.PrefetchScalarGridSpec(
            num_scalar_prefetch=1,
            grid=(HEADS // HG,),
            in_specs=[head_spec(HG), SECONDROWS, gain_spec(), gain_spec(), gain_spec()] + [message_spec()] * PEERS + [MSGTILE] * PEERS,
            out_specs=[message_spec()] * PEERS,
            scratch_shapes=[
                pltpu.VMEM((PEERS, HG * TOK, HDIM), BF),
                pltpu.VMEM((PEERS, HG * TOK, HDIM), BF),
                pltpu.VMEM((SEQ, HDIM), F32),
            ],
        ),
        out_shape=[jax.ShapeDtypeStruct((ROWS, HDIM), BF)] * PEERS,
        compiler_params=pltpu.CompilerParams(vmem_limit_bytes=24 * MIB),
        name="second_layer",
    )(meta, y, ss, qg, kg, vg, *fresh, *fresh)


def backward_kernel(meta_ref, g_ref, ss_ref, qg_ref, kg_ref, vg_ref, *rest):
    msgs = rest[:PEERS]
    tiles = rest[PEERS : 2 * PEERS]
    dn_ref, x_ref, factor_ref, in_ref = rest[2 * PEERS : 2 * PEERS + 4]
    in_scr, p_scr, ds_scr = rest[2 * PEERS + 4 :]
    h = pl.program_id(0)
    t = meta_ref[0]

    @pl.when(h == 0)
    def _():
        for k in range(PEERS):
            at = pl.multiple_of((t ^ k) * TOK, TOK)
            factor_ref[pl.ds(at, TOK), :] = factor_column(tiles[k][...])
        in_scr[...] = jnp.zeros_like(in_scr)

    for k in range(PEERS):
        x_ref[t ^ k] = msgs[k][...]
    for b in range(HG):
        rows, lanes = slice(b * TOK, (b + 1) * TOK), slice(b * HDIM, (b + 1) * HDIM)
        qg, kg, vg = qg_ref[:, lanes], kg_ref[:, lanes], vg_ref[:, lanes]
        x = x_ref[:, rows, :].reshape(SEQ, HDIM).astype(F32)
        g = g_ref[:, rows, :].reshape(SEQ, HDIM)
        scaled, q, k, v = heads_of(x, factor_ref[...], qg, kg, vg)
        dq = []
        for i in range(SEQ // QB):
            n = (i + 1) * QB
            p = probs_block(q, k, i)
            p_scr[b, i * QB : n, :n] = p.astype(BF)
            dp = dot(g[i * QB : n], v[:n], 1, 1)
            ds = (p * (dp - jnp.sum(dp * p, axis=1, keepdims=True))).astype(BF)
            ds_scr[b, i * QB : n, :n] = ds
            dq.append(dot(ds, k[:n], 1, 0))
        per = QB // TOK
        for j in range(SEQ // QB):
            lo, hi = j * QB, (j + 1) * QB
            dv = dot(p_scr[b, lo:, lo:hi], g[lo:], 0, 0)
            dk = dot(ds_scr[b, lo:, lo:hi], q[lo:], 0, 0)
            dn = dq[j] * SCALE * qg + dk * SCALE * kg + dv * vg
            dn = dn.astype(BF)
            dn_ref[j * per : (j + 1) * per, rows, :] = dn.reshape(per, TOK, HDIM)
            in_scr[lo:hi, :] += dn.astype(F32) * scaled[lo:hi]

    @pl.when(h == HEADS // HG - 1)
    def _():
        ones = jnp.ones((8, HDIM), F32)
        in_ref[0:8, :] = dot(ones, in_scr[...], 1, 1, lax.Precision.HIGHEST)
        in_ref[8:16, :] = ss_ref[...]


def backward_heads(meta, g, ss, msgs, qg, kg, vg):
    return pl.pallas_call(
        backward_kernel,
        grid_spec=pltpu.PrefetchScalarGridSpec(
            num_scalar_prefetch=1,
            grid=(HEADS // HG,),
            in_specs=[head_spec(HG, HEADS), ROWSPEC, gain_spec(), gain_spec(), gain_spec()] + [message_spec()] * PEERS + [MSGTILE] * PEERS,
            out_specs=[
                head_spec(HG),
                head_spec(HG),
                pl.BlockSpec((SEQ, HDIM), lambda h, *_: (0, 0)),
                BOTHROWS,
            ],
            scratch_shapes=[
                pltpu.VMEM((SEQ, HDIM), F32),
                pltpu.VMEM((HG, SEQ, SEQ), BF),
                pltpu.VMEM((HG, SEQ, SEQ), BF),
            ],
        ),
        out_shape=[
            jax.ShapeDtypeStruct((PEERS, ROWS, HDIM), BF),
            jax.ShapeDtypeStruct((PEERS, ROWS, HDIM), BF),
            jax.ShapeDtypeStruct((SEQ, HDIM), F32),
            jax.ShapeDtypeStruct((16, SEQ), F32),
        ],
        compiler_params=pltpu.CompilerParams(vmem_limit_bytes=28 * MIB),
        name="backward_heads",
    )(meta, g, ss, qg, kg, vg, *msgs, *msgs)


def finish_kernel(g_ref, dn_ref, x_ref, factor_ref, in_ref, out_ref, inner_scr):
    @pl.when(pl.program_id(0) == 0)
    def _():
        inner_scr[...] = column_of_rows(in_ref[...]) * (1.0 / D)

    factor = factor_ref[...]
    for b in range(FG):
        rows = slice(b * TOK, (b + 1) * TOK)
        a = x_ref[:, rows, :].reshape(SEQ, HDIM).astype(F32) * factor
        dn = dn_ref[:, rows, :].reshape(SEQ, HDIM).astype(F32)
        g = g_ref[:, rows, :].reshape(SEQ, HDIM).astype(F32)
        out = (g + factor * (dn - a * inner_scr[...])).astype(BF)
        out_ref[:, rows, :] = out.reshape(PEERS, TOK, HDIM)


def finish(g, dn, x, factor, inner):
    return pl.pallas_call(
        finish_kernel,
        grid=(HEADS // FG,),
        in_specs=[
            head_spec(FG, HEADS),
            head_spec(FG),
            head_spec(FG),
            pl.BlockSpec((SEQ, HDIM), lambda h: (0, 0)),
            ROWSPEC,
        ],
        out_specs=head_spec(FG),
        out_shape=jax.ShapeDtypeStruct((PEERS, ROWS, HDIM), BF),
        scratch_shapes=[pltpu.VMEM((SEQ, HDIM), F32)],
        compiler_params=pltpu.CompilerParams(vmem_limit_bytes=20 * MIB),
        name="finish",
    )(g, dn, x, factor, inner)


def copy_kernel(x_ref, out_ref):
    out_ref[...] = x_ref[...]


def copied(x):
    return pl.pallas_call(
        copy_kernel,
        out_shape=jax.ShapeDtypeStruct(x.shape, x.dtype),
        in_specs=[VMEM],
        out_specs=VMEM,
        compiler_params=pltpu.CompilerParams(vmem_limit_bytes=8 * MIB),
        name="copied",
    )(x)


def exchange(m):
    return lax.all_to_all(m, "tensor", split_axis=0, concat_axis=0, tiled=True)


def xor_moves(msgs, target, sources=range(SECTIONS)):
    out = []
    for k in range(PEERS):
        pairs = [
            (s * PEERS + t, target(s) * PEERS + (t ^ k)) for s in sources for t in range(PEERS)
        ]
        if all(a == b for a, b in pairs):
            out.append(msgs[k])
        else:
            out.append(lax.ppermute(msgs[k], BOTH, pairs))
    return out


def all_sum(v):
    for step in range(3):
        pairs = [(t, t ^ (1 << step)) for t in range(PEERS)]
        v = v + lax.ppermute(v, "tensor", pairs)
    return v


def device_program(inflow, fresh, stash_held, grad_in, query_gain, key_gain, value_gain):
    t = lax.axis_index("tensor").astype(jnp.int32)
    last = (lax.axis_index("section") == SECTIONS - 1).astype(jnp.int32)
    tvec = t[None]
    meta = jnp.stack([t, last])
    gains = jnp.concatenate([query_gain, key_gain, value_gain], axis=0)
    behind = [((s + 1) % SECTIONS, s) for s in range(SECTIONS)]
    ahead = lax.ppermute(gains, "section", behind)
    here = (query_gain, key_gain, value_gain)
    following = (ahead[0:1], ahead[1:2], ahead[2:3])
    mirror = [(s, SECTIONS - 1 - s) for s in range(SECTIONS)]

    wide = exchange(pack_wide(inflow[0], grad_in[0]))
    packed = pack_xor(tvec, stash_held[0])
    stash_msgs = xor_moves(packed, lambda s: SECTIONS - 1 - s)
    packed = pack_xor(tvec, fresh)
    fresh_msgs = xor_moves(packed, lambda s: s, (SECTIONS - 1,))
    evicted = copied(lax.ppermute(inflow, "section", mirror))

    y, ss = first_layer(wide, *here)
    first_out = unpack_natural(exchange(y))
    dn, xn, factor, sums = backward_heads(meta, wide, ss, stash_msgs, *here)
    sums = all_sum(sums)

    grad_heads = finish(wide, dn, xn, factor, sums)
    grad_out = unpack_natural(exchange(grad_heads))
    out_msgs = second_layer(meta, y, sums, *following, fresh_msgs)
    moved = xor_moves(out_msgs, lambda s: (s + 1) % SECTIONS)
    second_out = unpack_xor(tvec, moved)
    return (first_out, second_out, evicted, grad_out)


def solution(mesh):
    rows = P("section", "tensor", None)
    gain = P("section", "tensor")
    return jax.shard_map(
        device_program,
        mesh=mesh,
        in_specs=(rows, P("tensor", None), rows, rows, gain, gain, gain),
        out_specs=(rows, rows, rows, rows),
        check_vma=False,
    )
```

```python
import math

import jax
import jax.numpy as jnp
from jax import lax
from jax.experimental import pallas as pl
from jax.experimental.pallas import tpu as pltpu
from jax.sharding import PartitionSpec as P


D = 12288
HDIM = 128
SEQ = 512
SECTIONS = 16
PEERS = 8
TOK = SEQ // PEERS
HEADS = D // HDIM // PEERS
FEAT = HEADS * HDIM
ROWS = HEADS * TOK
MSG = ROWS + 8
QB = 512
HG = 4
FG = 6
CUTS = (0, 32, 64)
FRESH_FROM = (15, 7, 14, 6, 13, 5, 12, 4)
MIB = 1 << 20
EPS = 1e-05
NEG = -1e30
SCALE = HDIM**-0.5
EXPC = SCALE * math.log2(math.e)
BF = jnp.bfloat16
F32 = jnp.float32
BOTH = ("section", "tensor")
VMEM = pl.BlockSpec(memory_space=pltpu.VMEM)
SMEM = pl.BlockSpec(memory_space=pltpu.SMEM)


def dot(a, b, ca, cb, precision=None):
    return lax.dot_general(
        a, b, (((ca,), (cb,)), ((), ())), precision=precision, preferred_element_type=F32
    )


def stats_tile(x_ref):
    acc = jnp.zeros((TOK, HDIM), F32)
    for c in range(D // HDIM):
        v = x_ref[:, c * HDIM : (c + 1) * HDIM].astype(F32)
        acc = acc + v * v
    total = dot(jnp.ones((8, HDIM), F32), acc, 1, 1, lax.Precision.HIGHEST)
    hi = total.astype(BF).astype(F32)
    mid = (total - hi).astype(BF).astype(F32)
    low = total - hi - mid
    row = lax.broadcasted_iota(jnp.int32, (8, TOK), 0)
    pieces = jnp.where(row == 0, hi, jnp.where(row == 1, mid, jnp.where(row == 2, low, 0.0)))
    return jnp.concatenate([pieces, jnp.zeros((8, HDIM - TOK), F32)], axis=1).astype(BF)


def pack_natural_kernel(x_ref, out_ref):
    for u in range(PEERS):
        for h in range(HEADS):
            c = u * FEAT + h * HDIM
            out_ref[u, h * TOK : (h + 1) * TOK, :] = x_ref[:, c : c + HDIM]
    tile = stats_tile(x_ref)
    for u in range(PEERS):
        out_ref[u, ROWS:MSG, :] = tile


def pack_xor_kernel(t_ref, x_ref, *outs, stats):
    t = t_ref[0]
    if stats:
        tile = stats_tile(x_ref)
    for k in range(PEERS):
        base = (t ^ k) * FEAT
        for h in range(HEADS):
            c = pl.multiple_of(base + h * HDIM, HDIM)
            outs[k][h * TOK : (h + 1) * TOK, :] = x_ref[:, pl.ds(c, HDIM)]
        if stats:
            outs[k][ROWS:MSG, :] = tile


def pack_natural(x):
    return pl.pallas_call(
        pack_natural_kernel,
        out_shape=jax.ShapeDtypeStruct((PEERS, MSG, HDIM), BF),
        in_specs=[VMEM],
        out_specs=VMEM,
        compiler_params=pltpu.CompilerParams(vmem_limit_bytes=8 * MIB),
        name="pack_natural",
    )(x)


def pack_xor(t, x, stats=True):
    def body(*refs):
        pack_xor_kernel(*refs, stats=stats)

    return pl.pallas_call(
        body,
        out_shape=[jax.ShapeDtypeStruct((MSG if stats else ROWS, HDIM), BF)] * PEERS,
        in_specs=[SMEM, VMEM],
        out_specs=[VMEM] * PEERS,
        compiler_params=pltpu.CompilerParams(vmem_limit_bytes=8 * MIB),
        name="pack_xor",
    )(t, x)


def unpack_natural_kernel(m_ref, out_ref):
    for u in range(PEERS):
        for h in range(HEADS):
            c = u * FEAT + h * HDIM
            out_ref[0, :, c : c + HDIM] = m_ref[u, h * TOK : (h + 1) * TOK, :]


def unpack_xor_kernel(t_ref, *refs):
    t = t_ref[0]
    out_ref = refs[PEERS]
    for k in range(PEERS):
        base = (t ^ k) * FEAT
        for h in range(HEADS):
            c = pl.multiple_of(base + h * HDIM, HDIM)
            out_ref[0, :, pl.ds(c, HDIM)] = refs[k][h * TOK : (h + 1) * TOK, :]


def unpack_natural(m):
    return pl.pallas_call(
        unpack_natural_kernel,
        out_shape=jax.ShapeDtypeStruct((1, TOK, D), BF),
        in_specs=[VMEM],
        out_specs=VMEM,
        compiler_params=pltpu.CompilerParams(vmem_limit_bytes=8 * MIB),
        name="unpack_natural",
    )(m)


def unpack_xor(t, ms):
    return pl.pallas_call(
        unpack_xor_kernel,
        out_shape=jax.ShapeDtypeStruct((1, TOK, D), BF),
        in_specs=[SMEM] + [VMEM] * PEERS,
        out_specs=VMEM,
        compiler_params=pltpu.CompilerParams(vmem_limit_bytes=8 * MIB),
        name="unpack_xor",
    )(t, *ms)


def factor_column(tile):
    ones = jnp.ones((8, HDIM), BF)
    total = dot(tile, ones, 0, 0)
    return lax.rsqrt(total[:TOK] * (1.0 / D) + EPS)


def column_of_rows(rows):
    return dot(rows, jnp.full((8, HDIM), 0.125, F32), 0, 0, lax.Precision.HIGHEST)


def heads_of(x, factor, qg, kg, vg):
    scaled = x * factor
    normed = scaled.astype(BF).astype(F32)
    return scaled, (normed * qg).astype(BF), (normed * kg).astype(BF), (normed * vg).astype(BF)


def probs_block(q, k, i):
    n = (i + 1) * QB
    s = dot(q[i * QB : n], k[:n], 1, 1)
    row = lax.broadcasted_iota(jnp.int32, (QB, QB), 0)
    col = lax.broadcasted_iota(jnp.int32, (QB, QB), 1)
    last = jnp.where(row >= col, s[:, i * QB :], NEG)
    s = jnp.concatenate([s[:, : i * QB], last], axis=1) if i else last
    e = jnp.exp2((s - jnp.max(s, axis=1, keepdims=True)) * EXPC)
    return e * (1.0 / jnp.sum(e, axis=1, keepdims=True))


def attend(x, factor, qg, kg, vg, store):
    _, q, k, v = heads_of(x, factor, qg, kg, vg)
    for i in range(SEQ // QB):
        n = (i + 1) * QB
        p = probs_block(q, k, i).astype(BF)
        mixed = dot(p, v[:n], 1, 0).astype(BF).astype(F32)
        store(i, (x[i * QB : n] + mixed).astype(BF))


def first_kernel(x_ref, tile_ref, qg_ref, kg_ref, vg_ref, y_ref, ss_ref, factor_scr, sq_scr):
    h = pl.program_id(0)

    @pl.when(h == 0)
    def _():
        for u in range(PEERS):
            factor_scr[u * TOK : (u + 1) * TOK, :] = factor_column(tile_ref[u])
        sq_scr[...] = jnp.zeros_like(sq_scr)

    for b in range(HG):
        rows, lanes = slice(b * TOK, (b + 1) * TOK), slice(b * HDIM, (b + 1) * HDIM)
        x = x_ref[:, rows, :].reshape(SEQ, HDIM).astype(F32)

        def store(i, y):
            per = QB // TOK
            y_ref[i * per : (i + 1) * per, rows, :] = y.reshape(per, TOK, HDIM)
            yf = y.astype(F32)
            sq_scr[i * QB : (i + 1) * QB, :] += yf * yf

        attend(x, factor_scr[...], qg_ref[:, lanes], kg_ref[:, lanes], vg_ref[:, lanes], store)

    @pl.when(h == HEADS // HG - 1)
    def _():
        ss_ref[...] = dot(jnp.ones((8, HDIM), F32), sq_scr[...], 1, 1, lax.Precision.HIGHEST)


def gain_spec():
    return pl.BlockSpec((1, HG * HDIM), lambda h, *_: (0, h))


def head_spec(per):
    return pl.BlockSpec((PEERS, per * TOK, HDIM), lambda h, *_: (0, h, 0))


def message_spec():
    return pl.BlockSpec((HG * TOK, HDIM), lambda h, *_: (h, 0))


TILES = pl.BlockSpec((PEERS, 8, HDIM), lambda h, *_: (0, ROWS // 8, 0))
ROWSPEC = pl.BlockSpec((8, SEQ), lambda h, *_: (0, 0))
SECONDROWS = pl.BlockSpec((8, SEQ), lambda h, *_: (1, 0))
BOTHROWS = pl.BlockSpec((16, SEQ), lambda h, *_: (0, 0))
MSGTILE = pl.BlockSpec((8, HDIM), lambda h, *_: (ROWS // 8, 0))


def first_layer(xm, qg, kg, vg):
    return pl.pallas_call(
        first_kernel,
        grid=(HEADS // HG,),
        in_specs=[head_spec(HG), TILES, gain_spec(), gain_spec(), gain_spec()],
        out_specs=[head_spec(HG), ROWSPEC],
        out_shape=[
            jax.ShapeDtypeStruct((PEERS, ROWS, HDIM), BF),
            jax.ShapeDtypeStruct((8, SEQ), F32),
        ],
        scratch_shapes=[pltpu.VMEM((SEQ, HDIM), F32), pltpu.VMEM((SEQ, HDIM), F32)],
        compiler_params=pltpu.CompilerParams(vmem_limit_bytes=24 * MIB),
        name="first_layer",
    )(xm, xm, qg, kg, vg)


def second_kernel(
    meta_ref, y_ref, ss_ref, qg_ref, kg_ref, vg_ref, *rest
):
    fresh = rest[:PEERS]
    tiles = rest[PEERS : 2 * PEERS]
    outs = rest[2 * PEERS : 3 * PEERS]
    x_scr, out_scr, factor_scr = rest[3 * PEERS :]
    h = pl.program_id(0)
    t = meta_ref[0]
    last = meta_ref[1] == 1

    @pl.when(h == 0)
    def _():
        factor_scr[...] = lax.rsqrt(column_of_rows(ss_ref[...]) * (1.0 / D) + EPS)

    @pl.when(jnp.logical_and(h == 0, last))
    def _():
        for k in range(PEERS):
            at = pl.multiple_of((t ^ k) * TOK, TOK)
            factor_scr[pl.ds(at, TOK), :] = factor_column(tiles[k][...])

    @pl.when(jnp.logical_not(last))
    def _():
        x_scr[...] = y_ref[...]

    @pl.when(last)
    def _():
        for k in range(PEERS):
            x_scr[t ^ k] = fresh[k][...]

    for b in range(HG):
        rows, lanes = slice(b * TOK, (b + 1) * TOK), slice(b * HDIM, (b + 1) * HDIM)
        x = x_scr[:, rows, :].reshape(SEQ, HDIM).astype(F32)

        def store(i, y):
            per = QB // TOK
            out_scr[i * per : (i + 1) * per, rows, :] = y.reshape(per, TOK, HDIM)

        attend(x, factor_scr[...], qg_ref[:, lanes], kg_ref[:, lanes], vg_ref[:, lanes], store)
    for k in range(PEERS):
        outs[k][...] = out_scr[t ^ k]


def second_layer(meta, y, ss, qg, kg, vg, fresh):
    return pl.pallas_call(
        second_kernel,
        grid_spec=pltpu.PrefetchScalarGridSpec(
            num_scalar_prefetch=1,
            grid=(HEADS // HG,),
            in_specs=[head_spec(HG), SECONDROWS, gain_spec(), gain_spec(), gain_spec()] + [message_spec()] * PEERS + [MSGTILE] * PEERS,
            out_specs=[message_spec()] * PEERS,
            scratch_shapes=[
                pltpu.VMEM((PEERS, HG * TOK, HDIM), BF),
                pltpu.VMEM((PEERS, HG * TOK, HDIM), BF),
                pltpu.VMEM((SEQ, HDIM), F32),
            ],
        ),
        out_shape=[jax.ShapeDtypeStruct((ROWS, HDIM), BF)] * PEERS,
        compiler_params=pltpu.CompilerParams(vmem_limit_bytes=24 * MIB),
        name="second_layer",
    )(meta, y, ss, qg, kg, vg, *fresh, *fresh)


def backward_kernel(meta_ref, ss_ref, qg_ref, kg_ref, vg_ref, *rest):
    msgs = rest[:PEERS]
    tiles = rest[PEERS : 2 * PEERS]
    grads = rest[2 * PEERS : 3 * PEERS]
    dn_ref, x_ref, g_ref, factor_ref, in_ref = rest[3 * PEERS : 3 * PEERS + 5]
    in_scr, p_scr, ds_scr = rest[3 * PEERS + 5 :]
    h = pl.program_id(0)
    t = meta_ref[0]

    @pl.when(h == 0)
    def _():
        for k in range(PEERS):
            at = pl.multiple_of((t ^ k) * TOK, TOK)
            factor_ref[pl.ds(at, TOK), :] = factor_column(tiles[k][...])
        in_scr[...] = jnp.zeros_like(in_scr)

    for k in range(PEERS):
        x_ref[t ^ k] = msgs[k][...]
        g_ref[t ^ k] = grads[k][...]
    for b in range(HG):
        rows, lanes = slice(b * TOK, (b + 1) * TOK), slice(b * HDIM, (b + 1) * HDIM)
        qg, kg, vg = qg_ref[:, lanes], kg_ref[:, lanes], vg_ref[:, lanes]
        x = x_ref[:, rows, :].reshape(SEQ, HDIM).astype(F32)
        g = g_ref[:, rows, :].reshape(SEQ, HDIM)
        scaled, q, k, v = heads_of(x, factor_ref[...], qg, kg, vg)
        dq = []
        for i in range(SEQ // QB):
            n = (i + 1) * QB
            p = probs_block(q, k, i)
            p_scr[b, i * QB : n, :n] = p.astype(BF)
            dp = dot(g[i * QB : n], v[:n], 1, 1)
            ds = (p * (dp - jnp.sum(dp * p, axis=1, keepdims=True))).astype(BF)
            ds_scr[b, i * QB : n, :n] = ds
            dq.append(dot(ds, k[:n], 1, 0))
        per = QB // TOK
        for j in range(SEQ // QB):
            lo, hi = j * QB, (j + 1) * QB
            dv = dot(p_scr[b, lo:, lo:hi], g[lo:], 0, 0)
            dk = dot(ds_scr[b, lo:, lo:hi], q[lo:], 0, 0)
            dn = dq[j] * SCALE * qg + dk * SCALE * kg + dv * vg
            dn = dn.astype(BF)
            dn_ref[j * per : (j + 1) * per, rows, :] = dn.reshape(per, TOK, HDIM)
            in_scr[lo:hi, :] += dn.astype(F32) * scaled[lo:hi]

    @pl.when(h == HEADS // HG - 1)
    def _():
        ones = jnp.ones((8, HDIM), F32)
        in_ref[0:8, :] = dot(ones, in_scr[...], 1, 1, lax.Precision.HIGHEST)
        in_ref[8:16, :] = ss_ref[...]


def backward_heads(meta, grads, ss, msgs, qg, kg, vg):
    return pl.pallas_call(
        backward_kernel,
        grid_spec=pltpu.PrefetchScalarGridSpec(
            num_scalar_prefetch=1,
            grid=(HEADS // HG,),
            in_specs=[ROWSPEC, gain_spec(), gain_spec(), gain_spec()]
            + [message_spec()] * PEERS
            + [MSGTILE] * PEERS
            + [message_spec()] * PEERS,
            out_specs=[
                head_spec(HG),
                head_spec(HG),
                head_spec(HG),
                pl.BlockSpec((SEQ, HDIM), lambda h, *_: (0, 0)),
                BOTHROWS,
            ],
            scratch_shapes=[
                pltpu.VMEM((SEQ, HDIM), F32),
                pltpu.VMEM((HG, SEQ, SEQ), BF),
                pltpu.VMEM((HG, SEQ, SEQ), BF),
            ],
        ),
        out_shape=[
            jax.ShapeDtypeStruct((PEERS, ROWS, HDIM), BF),
            jax.ShapeDtypeStruct((PEERS, ROWS, HDIM), BF),
            jax.ShapeDtypeStruct((PEERS, ROWS, HDIM), BF),
            jax.ShapeDtypeStruct((SEQ, HDIM), F32),
            jax.ShapeDtypeStruct((16, SEQ), F32),
        ],
        compiler_params=pltpu.CompilerParams(vmem_limit_bytes=28 * MIB),
        name="backward_heads",
    )(meta, ss, qg, kg, vg, *msgs, *msgs, *grads)


def finish_kernel(g_ref, dn_ref, x_ref, factor_ref, in_ref, out_ref, inner_scr):
    @pl.when(pl.program_id(0) == 0)
    def _():
        inner_scr[...] = column_of_rows(in_ref[...]) * (1.0 / D)

    factor = factor_ref[...]
    for b in range(FG):
        rows = slice(b * TOK, (b + 1) * TOK)
        a = x_ref[:, rows, :].reshape(SEQ, HDIM).astype(F32) * factor
        dn = dn_ref[:, rows, :].reshape(SEQ, HDIM).astype(F32)
        g = g_ref[:, rows, :].reshape(SEQ, HDIM).astype(F32)
        out = (g + factor * (dn - a * inner_scr[...])).astype(BF)
        out_ref[:, rows, :] = out.reshape(PEERS, TOK, HDIM)


def finish(g, dn, x, factor, inner):
    return pl.pallas_call(
        finish_kernel,
        grid=(HEADS // FG,),
        in_specs=[
            head_spec(FG),
            head_spec(FG),
            head_spec(FG),
            pl.BlockSpec((SEQ, HDIM), lambda h: (0, 0)),
            ROWSPEC,
        ],
        out_specs=head_spec(FG),
        out_shape=jax.ShapeDtypeStruct((PEERS, ROWS, HDIM), BF),
        scratch_shapes=[pltpu.VMEM((SEQ, HDIM), F32)],
        compiler_params=pltpu.CompilerParams(vmem_limit_bytes=20 * MIB),
        name="finish",
    )(g, dn, x, factor, inner)


def join_kernel(*refs):
    out_ref = refs[-1]
    for i in range(len(CUTS) - 1):
        out_ref[0, CUTS[i] : CUTS[i + 1], :] = refs[i][0]


def joined(*parts):
    return pl.pallas_call(
        join_kernel,
        out_shape=jax.ShapeDtypeStruct((1, TOK, D), BF),
        in_specs=[VMEM] * len(parts),
        out_specs=VMEM,
        compiler_params=pltpu.CompilerParams(vmem_limit_bytes=8 * MIB),
        name="joined",
    )(*parts)


def exchange(m):
    return lax.all_to_all(m, "tensor", split_axis=0, concat_axis=0, tiled=True)


def xor_moves(msgs, target):
    out = []
    for k in range(PEERS):
        pairs = [
            (s * PEERS + t, target(s) * PEERS + (t ^ k))
            for s in range(SECTIONS)
            for t in range(PEERS)
        ]
        if all(a == b for a, b in pairs):
            out.append(msgs[k])
        else:
            out.append(lax.ppermute(msgs[k], BOTH, pairs))
    return out


def fresh_moves(msgs):
    out = [msgs[0]]
    for k in range(1, PEERS):
        source, target = FRESH_FROM[k] * PEERS, (SECTIONS - 1) * PEERS
        pairs = [(source + t, target + (t ^ k)) for t in range(PEERS)]
        out.append(lax.ppermute(msgs[k], BOTH, pairs))
    return out


def all_sum(v):
    for step in range(3):
        pairs = [(t, t ^ (1 << step)) for t in range(PEERS)]
        v = v + lax.ppermute(v, "tensor", pairs)
    return v


def device_program(inflow, fresh, stash_held, grad_in, query_gain, key_gain, value_gain):
    t = lax.axis_index("tensor").astype(jnp.int32)
    last = (lax.axis_index("section") == SECTIONS - 1).astype(jnp.int32)
    tvec = t[None]
    meta = jnp.stack([t, last])
    gains = jnp.concatenate([query_gain, key_gain, value_gain], axis=0)
    behind = [((s + 1) % SECTIONS, s) for s in range(SECTIONS)]
    ahead = lax.ppermute(gains, "section", behind)
    here = (query_gain, key_gain, value_gain)
    following = (ahead[0:1], ahead[1:2], ahead[2:3])
    mirror = [(s, SECTIONS - 1 - s) for s in range(SECTIONS)]

    xm = exchange(pack_natural(inflow[0]))
    packed = pack_xor(tvec, stash_held[0])
    stash_msgs = xor_moves(packed, lambda s: SECTIONS - 1 - s)
    packed = pack_xor(tvec, grad_in[0], False)
    grads = xor_moves(packed, lambda s: s)
    packed = pack_xor(tvec, fresh)
    fresh_msgs = fresh_moves(packed)
    parts = [inflow[:, CUTS[i] : CUTS[i + 1]] for i in range(len(CUTS) - 1)]
    parts = [lax.ppermute(p, "section", mirror) for p in parts]
    evicted = joined(*parts)

    y, ss = first_layer(xm, *here)
    first_out = unpack_natural(exchange(y))
    dn, xn, gn, factor, sums = backward_heads(meta, grads, ss, stash_msgs, *here)
    sums = all_sum(sums)

    grad_heads = finish(gn, dn, xn, factor, sums)
    grad_out = unpack_natural(exchange(grad_heads))
    out_msgs = second_layer(meta, y, sums, *following, fresh_msgs)
    moved = xor_moves(out_msgs, lambda s: (s + 1) % SECTIONS)
    second_out = unpack_xor(tvec, moved)
    return (first_out, second_out, evicted, grad_out)


def solution(mesh):
    rows = P("section", "tensor", None)
    gain = P("section", "tensor")
    return jax.shard_map(
        device_program,
        mesh=mesh,
        in_specs=(rows, P("tensor", None), rows, rows, gain, gain, gain),
        out_specs=(rows, rows, rows, rows),
        check_vma=False,
    )
```
